32 devices in a mesh: row: 8 (over z, y), col: 4 (over x, core).
Axes of the slice: x: 2, y: 2, z: 4, core: 2. Of those that a mesh axis runs over, the one named last changes fastest.
Arguments:
- tokens_in: bfloat16 [192, 8192], P('row', 'col'), may hold values from -6 to 6
- gate_weight: bfloat16 [8192, 28672], P('col', 'row'), may hold values from -0.0625 to 0.0625
- up_weight: bfloat16 [8192, 28672], P('col', 'row'), may hold values from -0.0625 to 0.0625
- down_weight: bfloat16 [28672, 8192], P('row', 'col'), may hold values from -0.03125 to 0.03125
- out_grad: bfloat16 [192, 8192], P('row', 'col'), may hold values from -0.29882812 to 0.29882812
Outputs:
- output: bfloat16 [192, 8192], P('row', 'col')
- in_grad: bfloat16 [192, 8192], P('row', 'col')
- gate_grad: bfloat16 [8192, 28672], P('col', 'row')
- up_grad: bfloat16 [8192, 28672], P('col', 'row')
- down_grad: bfloat16 [28672, 8192], P('row', 'col')
The draws below stay inside these ranges and needn't reach their ends.
All inputs are finite; a program needn't handle non-finite values.
Results may differ from the reference program's by a relative error of at most 0.0051.
Values may be sent and summed in bfloat16 or wider, within the bound.
A program may use at most 192 MiB of HBM per device.

```python
import jax
import jax.numpy as jnp

D = 8192
FF = 28672
TOKENS = 192


def block_scale(rng, dims, split, low, largest):
    loudness, own = 1.0, jax.random.fold_in(rng, 6)
    for dim, blocks in split:
        draws = jnp.exp(jax.random.uniform(jax.random.fold_in(own, dim), (blocks,), jnp.float32, low / len(split), largest / len(split)))
        loudness = loudness * jnp.repeat(draws, dims[dim] // blocks).reshape([-1 if axis == dim else 1 for axis in range(len(dims))])
    return loudness


def scatter_about(stream_key, extent, spread, reach, shards=(), dtype=jnp.bfloat16):
    array = jax.random.normal(stream_key, extent, jnp.float32) * spread
    if len(shards) > 0:
        array = block_scale(stream_key, extent, shards, -0.22, 0.18) * array
    return jnp.clip(array, min=-reach, max=reach).astype(dtype)


def setup_inputs(seed: int = 0) -> dict:
    key_list = jax.random.split(jax.random.key(seed), 6)
    return {
        "tokens_in": scatter_about(key_list[0], (TOKENS, D), 1.0, 6.0, ((0, 8), (1, 4))),
        "gate_weight": scatter_about(key_list[1], (D, FF), D ** -0.5, 0.0625, ((0, 4), (1, 8))),
        "up_weight": scatter_about(key_list[2], (D, FF), D ** -0.5, 0.0625, ((0, 4), (1, 8))),
        "down_weight": scatter_about(key_list[3], (FF, D), FF ** -0.5, 0.03125, ((0, 8), (1, 4))),
        "out_grad": scatter_about(key_list[4], (TOKENS, D), 0.05, 0.29882812, ((0, 8), (1, 4))),
    }


def reference(tokens_in, gate_weight, up_weight, down_weight, out_grad):
    gate_pre = jnp.dot(tokens_in, gate_weight, preferred_element_type=jnp.float32)
    up_pre = jnp.dot(tokens_in, up_weight, preferred_element_type=jnp.float32)
    sigma_gate = jax.nn.sigmoid(gate_pre)
    activated = gate_pre * sigma_gate
    hidden = (activated * up_pre).astype(jnp.bfloat16)
    output = jnp.dot(hidden, down_weight, preferred_element_type=jnp.float32).astype(jnp.bfloat16)
    d_hidden = jnp.dot(out_grad, down_weight.T, preferred_element_type=jnp.float32)
    d_gate = (d_hidden * up_pre * sigma_gate * (1.0 + gate_pre * (1.0 - sigma_gate))).astype(jnp.bfloat16)
    d_up = (d_hidden * activated).astype(jnp.bfloat16)
    in_grad = (jnp.dot(d_gate, gate_weight.T, preferred_element_type=jnp.float32)
               + jnp.dot(d_up, up_weight.T, preferred_element_type=jnp.float32)).astype(jnp.bfloat16)
    gate_grad = jnp.dot(tokens_in.T, d_gate, preferred_element_type=jnp.float32).astype(jnp.bfloat16)
    up_grad = jnp.dot(tokens_in.T, d_up, preferred_element_type=jnp.float32).astype(jnp.bfloat16)
    down_grad = jnp.dot(hidden.T, out_grad, preferred_element_type=jnp.float32).astype(jnp.bfloat16)
    return (output, in_grad, gate_grad, up_grad, down_grad)
```

```python
import functools

import jax
import jax.numpy as jnp
from jax import lax
from jax.experimental import pallas as pl
from jax.experimental.pallas import tpu as pltpu
from jax.sharding import PartitionSpec as P

BF16 = jnp.bfloat16


def contract_last(left, right):
    return lax.dot_general(
        left, right, (((1,), (1,)), ((), ())), preferred_element_type=jnp.float32
    )


def contract_first(left, right):
    return lax.dot_general(
        left, right, (((0,), (0,)), ((), ())), preferred_element_type=jnp.float32
    )


def contract_mid(left, right):
    return jnp.dot(left, right, preferred_element_type=jnp.float32)


def tile_of(size, most):
    best = size
    for tile in range(128, most + 1, 128):
        if size % tile == 0:
            best = tile
    return best


def weight_grad_kernel(left_ref, right_ref, out_ref):
    out_ref[...] = jnp.dot(
        left_ref[...], right_ref[...], preferred_element_type=jnp.float32
    ).astype(out_ref.dtype)


def weight_grad(left_t, right):
    rows, tokens = left_t.shape
    cols = right.shape[1]
    tile = tile_of(cols, 512)
    return pl.pallas_call(
        weight_grad_kernel,
        grid=(cols // tile,),
        in_specs=[
            pl.BlockSpec((rows, tokens), lambda i: (0, 0)),
            pl.BlockSpec((tokens, tile), lambda i: (0, i)),
        ],
        out_specs=pl.BlockSpec((rows, tile), lambda i: (0, i)),
        out_shape=jax.ShapeDtypeStruct((rows, cols), BF16),
        cost_estimate=pl.CostEstimate(
            flops=2 * tokens * rows * cols,
            bytes_accessed=2 * (tokens * rows + tokens * cols + rows * cols),
            transcendentals=0,
        ),
    )(left_t, right)


def gather_kernel(n_z, n_y, cores, *refs):
    count = (len(refs) - 7) // 2
    ins, outs = refs[:count], refs[count : 2 * count]
    own_sem, up_send, up_recv, down_send, down_recv, y_send, y_recv = refs[2 * count :]
    row = lax.axis_index("row")
    core = lax.rem(lax.axis_index("col"), cores)
    z, y = row // n_y, lax.rem(row, n_y)
    peers = [lax.rem(y + step, n_y) for step in range(1, n_y)]
    barrier = pltpu.get_barrier_semaphore()

    def greet(z_to, y_to):
        pl.semaphore_signal(
            barrier, inc=1, device_id={"row": z_to * n_y + y_to}, device_id_type=pl.DeviceIdType.MESH
        )

    @pl.when(z < n_z - 1)
    def _():
        greet(z + 1, y)

    @pl.when(z > 0)
    def _():
        greet(z - 1, y)

    for peer in peers:
        greet(z, peer)

    ends = jnp.where(z > 0, 1, 0) + jnp.where(z < n_z - 1, 1, 0)
    pl.semaphore_wait(barrier, ends + len(peers))

    def slot(z_of, y_of):
        return lax.rem(y_of + core * (n_y // 2), n_y) * n_z + z_of

    def copy(item, source, z_of, sems, z_to, y_to):
        target = outs[item].at[slot(z_of, y)]
        return pltpu.make_async_remote_copy(
            src_ref=target if source is None else source,
            dst_ref=target,
            send_sem=sems[0],
            recv_sem=sems[1],
            device_id={"row": z_to * n_y + y_to},
            device_id_type=pl.DeviceIdType.MESH,
        )

    def up(item, step):
        source = ins[item] if step == 0 else None
        sems = (up_send.at[item, step], up_recv.at[item, step])
        return copy(item, source, z - step, sems, z + 1, y)

    def down(item, step):
        source = ins[item] if step == 0 else None
        sems = (down_send.at[item, step], down_recv.at[item, step])
        return copy(item, source, z + step, sems, z - 1, y)

    def across(item, offset, z_of, own):
        source = ins[item] if own else None
        place = lax.rem(z_of + n_z, n_z)
        sems = (y_send.at[item, offset, place], y_recv.at[item, offset, place])
        return copy(item, source, z_of, sems, z, peers[offset])

    def sends(item, step, act):
        @pl.when((z < n_z - 1) & (z >= step))
        def _():
            act(up(item, step))

        @pl.when((z > 0) & (z + step <= n_z - 1))
        def _():
            act(down(item, step))

        for offset in range(n_y - 1):
            if step == 0:
                act(across(item, offset, z, True))
            else:

                @pl.when(z >= step)
                def _():
                    act(across(item, offset, z - step, False))

                @pl.when(z + step <= n_z - 1)
                def _():
                    act(across(item, offset, z + step, False))

    local = [
        pltpu.make_async_copy(ins[item], outs[item].at[slot(z, y)], own_sem.at[item])
        for item in range(count)
    ]
    for item in range(count):
        sends(item, 0, lambda c: c.start())
        local[item].start()
    for item in range(count):
        for step in range(1, n_z):

            @pl.when(z >= step)
            def _():
                up(item, step - 1).wait_recv()

            @pl.when(z + step <= n_z - 1)
            def _():
                down(item, step - 1).wait_recv()

            sends(item, step, lambda c: c.start())
    for item in range(count):
        local[item].wait()
        for offset in range(n_y - 1):
            for z_of in range(n_z):
                across(item, offset, z_of, False).wait_recv()
        for step in range(n_z):
            sends(item, step, lambda c: c.wait_send())


def gather_rows(n_z, n_y, cores, *arrays):
    count = len(arrays)
    line = pltpu.SemaphoreType.DMA((count, n_z))
    side = pltpu.SemaphoreType.DMA((count, n_y, n_z))
    shape = arrays[0].shape
    out = pl.pallas_call(
        functools.partial(gather_kernel, n_z, n_y, cores),
        out_shape=[jax.ShapeDtypeStruct((n_z * n_y,) + shape, a.dtype) for a in arrays],
        in_specs=[pl.BlockSpec(memory_space=pl.ANY)] * count,
        out_specs=[pl.BlockSpec(memory_space=pl.ANY)] * count,
        scratch_shapes=[pltpu.SemaphoreType.DMA((count,)), line, line, line, line, side, side],
        compiler_params=pltpu.CompilerParams(collective_id=0, has_side_effects=True),
    )(*arrays)
    return [value.reshape(-1, shape[1]) for value in out]


def make_shards(n_row, n_col):
    cores = 2 if n_col % 2 == 0 else 1
    n_x = n_col // cores
    n_y = n_x if n_row % n_x == 0 and n_x % 2 == 0 else (2 if n_row % 2 == 0 else 1)
    n_z = n_row // n_y
    half = cores == 2 and n_y % 2 == 0

    def row_swap(value, bit):
        return lax.ppermute(value, "row", [(r, r ^ bit) for r in range(n_row)])

    def x_move(value, step):
        pairs = [
            (x * cores + k, (x + step) % n_x * cores + k) for x in range(n_x) for k in range(cores)
        ]
        return lax.ppermute(value, "col", pairs)

    def core_move(value):
        pairs = [(x * cores + k, x * cores + 1 - k) for x in range(n_x) for k in range(cores)]
        return lax.ppermute(value, "col", pairs)

    def scatter_row(total):
        row = lax.axis_index("row")
        core = lax.rem(lax.axis_index("col"), cores)
        z, y = row // n_y, lax.rem(row, n_y)
        slot = lax.rem(y + core * (n_y // 2), n_y) * n_z + z
        bit = n_row // 2
        while bit:
            rows = total.shape[0] // 2
            side = (slot // bit) % 2
            keep = lax.dynamic_slice_in_dim(total, side * rows, rows)
            send = lax.dynamic_slice_in_dim(total, (1 - side) * rows, rows).astype(BF16)
            move = bit // n_z if bit >= n_z else bit * n_y
            total = keep + row_swap(send, move).astype(jnp.float32)
            bit //= 2
        return total.astype(BF16)

    def sum_core(part):
        if cores == 1:
            return part
        if half:
            rows = part.shape[0] // 2
            return part[:rows] + core_move(part[rows:].astype(BF16)).astype(jnp.float32)
        return part + core_move(part)

    def sum_x(mine):
        sent = mine.astype(BF16)
        total = mine
        for step in range(1, n_x):
            total = total + x_move(sent, step).astype(jnp.float32)
        return total

    def gather_core(share):
        return jnp.concatenate([share, core_move(share)], axis=0) if half else share

    def shards(tokens_in, gate_weight, up_weight, down_weight, out_grad):
        inputs_all, grad_all = gather_rows(n_z, n_y, cores, tokens_in, out_grad)
        gate_part = contract_mid(inputs_all, gate_weight)
        inputs_all, gate_part = lax.optimization_barrier((inputs_all, gate_part))
        gate_pre = sum_x(sum_core(gate_part))
        up_part = contract_mid(inputs_all, up_weight)
        grad_all, up_part = lax.optimization_barrier((grad_all, up_part))
        up_pre = sum_x(sum_core(up_part))
        d_hidden = sum_core(contract_last(grad_all, down_weight))
        d_hidden_sent, d_hidden = d_hidden.astype(BF16), d_hidden
        moved = [x_move(d_hidden_sent, step) for step in range(1, n_x)]
        inputs_t = inputs_all.T
        sigma = jax.nn.sigmoid(gate_pre)
        activated = gate_pre * sigma
        hidden = gather_core((activated * up_pre).astype(BF16))
        output_part = contract_mid(hidden, down_weight)
        down_grad = contract_first(hidden, grad_all).astype(BF16)
        moved, output_part, down_grad = lax.optimization_barrier((moved, output_part, down_grad))
        for value in moved:
            d_hidden = d_hidden + value.astype(jnp.float32)
        d_gate = (d_hidden * up_pre * sigma * (1.0 + gate_pre * (1.0 - sigma))).astype(BF16)
        d_up = (d_hidden * activated).astype(BF16)
        d_gate, d_up = gather_core(d_gate), gather_core(d_up)
        output = scatter_row(output_part)
        in_part = contract_last(d_gate, gate_weight) + contract_last(d_up, up_weight)
        in_part, d_gate, d_up = lax.optimization_barrier((in_part, d_gate, d_up))
        in_grad = scatter_row(in_part)
        gate_grad = weight_grad(inputs_t, d_gate)
        up_grad = weight_grad(inputs_t, d_up)
        return (output, in_grad, gate_grad, up_grad, down_grad)

    return shards


def solution(mesh):
    in_specs = (P("row", "col"), P("col", "row"), P("col", "row"), P("row", "col"), P("row", "col"))
    out_specs = (
        P("row", "col"),
        P("row", "col"),
        P("col", "row"),
        P("col", "row"),
        P("row", "col"),
    )
    shards = make_shards(mesh.shape["row"], mesh.shape["col"])
    return jax.shard_map(shards, mesh=mesh, in_specs=in_specs, out_specs=out_specs, check_vma=False)
```

```python
import functools

import jax
import jax.numpy as jnp
from jax import lax
from jax.experimental import pallas as pl
from jax.experimental.pallas import tpu as pltpu
from jax.sharding import PartitionSpec as P

BF16 = jnp.bfloat16


def contract_last(left, right):
    return lax.dot_general(
        left, right, (((1,), (1,)), ((), ())), preferred_element_type=jnp.float32
    )


def contract_first(left, right):
    return lax.dot_general(
        left, right, (((0,), (0,)), ((), ())), preferred_element_type=jnp.float32
    )


def contract_mid(left, right):
    return jnp.dot(left, right, preferred_element_type=jnp.float32)


def tile_of(size, most):
    best = size
    for tile in range(128, most + 1, 128):
        if size % tile == 0:
            best = tile
    return best


def weight_grad_kernel(left_ref, right_ref, out_ref):
    out_ref[...] = jnp.dot(
        left_ref[...], right_ref[...], preferred_element_type=jnp.float32
    ).astype(out_ref.dtype)


def weight_grad(left_t, right):
    rows, tokens = left_t.shape
    cols = right.shape[1]
    tile = tile_of(cols, 256)
    return pl.pallas_call(
        weight_grad_kernel,
        grid=(cols // tile,),
        in_specs=[
            pl.BlockSpec((rows, tokens), lambda i: (0, 0)),
            pl.BlockSpec((tokens, tile), lambda i: (0, i)),
        ],
        out_specs=pl.BlockSpec((rows, tile), lambda i: (0, i)),
        out_shape=jax.ShapeDtypeStruct((rows, cols), BF16),
        cost_estimate=pl.CostEstimate(
            flops=2 * tokens * rows * cols,
            bytes_accessed=2 * (tokens * rows + tokens * cols + rows * cols),
            transcendentals=0,
        ),
    )(left_t, right)


def gather_kernel(n_z, n_y, cores, *refs):
    count = (len(refs) - 7) // 2
    ins, outs = refs[:count], refs[count : 2 * count]
    own_sem, up_send, up_recv, down_send, down_recv, y_send, y_recv = refs[2 * count :]
    row = lax.axis_index("row")
    core = lax.rem(lax.axis_index("col"), cores)
    z, y = row // n_y, lax.rem(row, n_y)
    peers = [lax.rem(y + step, n_y) for step in range(1, n_y)]
    barrier = pltpu.get_barrier_semaphore()

    def greet(z_to, y_to):
        pl.semaphore_signal(
            barrier, inc=1, device_id={"row": z_to * n_y + y_to}, device_id_type=pl.DeviceIdType.MESH
        )

    @pl.when(z < n_z - 1)
    def _():
        greet(z + 1, y)

    @pl.when(z > 0)
    def _():
        greet(z - 1, y)

    for peer in peers:
        greet(z, peer)

    ends = jnp.where(z > 0, 1, 0) + jnp.where(z < n_z - 1, 1, 0)
    pl.semaphore_wait(barrier, ends + len(peers))

    def slot(z_of, y_of):
        return lax.rem(y_of + core * (n_y // 2), n_y) * n_z + z_of

    def copy(item, source, z_of, sems, z_to, y_to):
        target = outs[item].at[slot(z_of, y)]
        return pltpu.make_async_remote_copy(
            src_ref=target if source is None else source,
            dst_ref=target,
            send_sem=sems[0],
            recv_sem=sems[1],
            device_id={"row": z_to * n_y + y_to},
            device_id_type=pl.DeviceIdType.MESH,
        )

    def up(item, step):
        source = ins[item] if step == 0 else None
        sems = (up_send.at[item, step], up_recv.at[item, step])
        return copy(item, source, z - step, sems, z + 1, y)

    def down(item, step):
        source = ins[item] if step == 0 else None
        sems = (down_send.at[item, step], down_recv.at[item, step])
        return copy(item, source, z + step, sems, z - 1, y)

    def across(item, offset, z_of, own):
        source = ins[item] if own else None
        place = lax.rem(z_of + n_z, n_z)
        sems = (y_send.at[item, offset, place], y_recv.at[item, offset, place])
        return copy(item, source, z_of, sems, z, peers[offset])

    def sends(item, step, act):
        @pl.when((z < n_z - 1) & (z >= step))
        def _():
            act(up(item, step))

        @pl.when((z > 0) & (z + step <= n_z - 1))
        def _():
            act(down(item, step))

        for offset in range(n_y - 1):
            if step == 0:
                act(across(item, offset, z, True))
            else:

                @pl.when(z >= step)
                def _():
                    act(across(item, offset, z - step, False))

                @pl.when(z + step <= n_z - 1)
                def _():
                    act(across(item, offset, z + step, False))

    local = [
        pltpu.make_async_copy(ins[item], outs[item].at[slot(z, y)], own_sem.at[item])
        for item in range(count)
    ]
    for item in range(count):
        sends(item, 0, lambda c: c.start())
        local[item].start()
    for item in range(count):
        for step in range(1, n_z):

            @pl.when(z >= step)
            def _():
                up(item, step - 1).wait_recv()

            @pl.when(z + step <= n_z - 1)
            def _():
                down(item, step - 1).wait_recv()

            sends(item, step, lambda c: c.start())
    for item in range(count):
        local[item].wait()
        for offset in range(n_y - 1):
            for z_of in range(n_z):
                across(item, offset, z_of, False).wait_recv()
        for step in range(n_z):
            sends(item, step, lambda c: c.wait_send())


def gather_rows(n_z, n_y, cores, call, *arrays):
    count = len(arrays)
    line = pltpu.SemaphoreType.DMA((count, n_z))
    side = pltpu.SemaphoreType.DMA((count, n_y, n_z))
    shape = arrays[0].shape
    out = pl.pallas_call(
        functools.partial(gather_kernel, n_z, n_y, cores),
        out_shape=[jax.ShapeDtypeStruct((n_z * n_y,) + shape, a.dtype) for a in arrays],
        in_specs=[pl.BlockSpec(memory_space=pl.ANY)] * count,
        out_specs=[pl.BlockSpec(memory_space=pl.ANY)] * count,
        scratch_shapes=[pltpu.SemaphoreType.DMA((count,)), line, line, line, line, side, side],
        cost_estimate=pl.CostEstimate(
            flops=0, bytes_accessed=8 * n_z * n_y * count * arrays[0].size, transcendentals=0
        ),
        compiler_params=pltpu.CompilerParams(collective_id=call, has_side_effects=True),
    )(*arrays)
    return [value.reshape(-1, shape[1]) for value in out]


def make_shards(n_row, n_col):
    cores = 2 if n_col % 2 == 0 else 1
    n_x = n_col // cores
    n_y = n_x if n_row % n_x == 0 and n_x % 2 == 0 else (2 if n_row % 2 == 0 else 1)
    n_z = n_row // n_y
    half = cores == 2 and n_y % 2 == 0

    def row_swap(value, bit):
        return lax.ppermute(value, "row", [(r, r ^ bit) for r in range(n_row)])

    def x_move(value, step):
        pairs = [
            (x * cores + k, (x + step) % n_x * cores + k) for x in range(n_x) for k in range(cores)
        ]
        return lax.ppermute(value, "col", pairs)

    def core_move(value):
        pairs = [(x * cores + k, x * cores + 1 - k) for x in range(n_x) for k in range(cores)]
        return lax.ppermute(value, "col", pairs)

    def scatter_start(total, bit):
        row = lax.axis_index("row")
        core = lax.rem(lax.axis_index("col"), cores)
        z, y = row // n_y, lax.rem(row, n_y)
        slot = lax.rem(y + core * (n_y // 2), n_y) * n_z + z
        rows = total.shape[0] // 2
        side = (slot // bit) % 2
        keep = lax.dynamic_slice_in_dim(total, side * rows, rows)
        send = lax.dynamic_slice_in_dim(total, (1 - side) * rows, rows).astype(BF16)
        return keep, row_swap(send, bit // n_z if bit >= n_z else bit * n_y)

    def gather_step(value, bit):
        arrived = row_swap(value, bit // n_z if bit >= n_z else bit * n_y)

        def both(arrived):
            row = lax.axis_index("row")
            core = lax.rem(lax.axis_index("col"), cores)
            slot = lax.rem(lax.rem(row, n_y) + core * (n_y // 2), n_y) * n_z + row // n_y
            lower = (slot // bit) % 2 == 0
            return jnp.concatenate(
                [jnp.where(lower, value, arrived), jnp.where(lower, arrived, value)], axis=0
            )

        return arrived, both

    def scatter_until(total, bit, last):
        while True:
            keep, arrived = scatter_start(total, bit)
            if bit == last:
                return keep, arrived
            total = keep + arrived.astype(jnp.float32)
            bit //= 2

    def sum_core(part, dtype):
        if cores == 1:
            return part
        if half:
            rows = part.shape[0] // 2
            return part[:rows] + core_move(part[rows:].astype(dtype)).astype(jnp.float32)
        return part + core_move(part)

    def send_x(mine):
        return [x_move(mine, step) for step in range(1, n_x)]

    def add_all(mine, moved):
        for value in moved:
            mine = mine + value.astype(jnp.float32)
        return mine

    def join(share, moved):
        return share if moved is None else jnp.concatenate([share, moved], axis=0)

    def core_send(share):
        return core_move(share) if half else None

    tie = lax.optimization_barrier

    def shards(tokens_in, gate_weight, up_weight, down_weight, out_grad):
        (inputs_all,) = gather_rows(n_z, n_y, cores, 0, tokens_in)
        inputs_all, out_grad = tie((inputs_all, out_grad))
        arrived, both = gather_step(out_grad, 1)
        gate_part = contract_mid(inputs_all, gate_weight)
        inputs_all, gate_part, arrived = tie((inputs_all, gate_part, arrived))
        grad_all, bit = both(arrived), 2
        arrived, both = gather_step(grad_all, bit)
        gate_mine = sum_core(gate_part, BF16)
        gate_moved = send_x(gate_mine.astype(BF16))
        up_mine = sum_core(contract_mid(inputs_all, up_weight), jnp.float32)
        arrived, up_sent = tie((arrived, up_mine.astype(BF16)))
        up_moved = send_x(up_sent)
        grad_all = both(arrived)
        while bit < n_row // 2:
            bit *= 2
            arrived, both = gather_step(grad_all, bit)
            grad_all = both(arrived)
        d_part = contract_last(grad_all, down_weight)
        d_mine = sum_core(d_part, jnp.float32)
        d_sent, gate_moved, up_moved, inputs_t = tie(
            (d_mine.astype(BF16), gate_moved, up_moved, inputs_all.T)
        )
        d_moved = send_x(d_sent)
        gate_pre, up_pre = add_all(gate_mine, gate_moved), add_all(up_mine, up_moved)
        sigma = jax.nn.sigmoid(gate_pre)
        activated = gate_pre * sigma
        share = (activated * up_pre).astype(BF16)
        hidden = join(share, core_send(share))
        output_part = contract_mid(hidden, down_weight)
        d_moved, output_part = tie((d_moved, output_part))
        out_keep, out_moved = scatter_until(output_part, n_row // 2, max(n_z, 1))
        d_hidden = add_all(d_mine, d_moved)
        d_gate = (d_hidden * up_pre * sigma * (1.0 + gate_pre * (1.0 - sigma))).astype(BF16)
        d_up = (d_hidden * activated).astype(BF16)
        d_gate, d_up, hidden = tie((d_gate, d_up, hidden))
        d_gate_moved, d_up_moved = core_send(d_gate), core_send(d_up)
        down_grad = contract_first(hidden, grad_all).astype(BF16)
        d_gate_moved, d_up_moved, out_moved, down_grad = tie(
            (d_gate_moved, d_up_moved, out_moved, down_grad)
        )
        d_gate, d_up = join(d_gate, d_gate_moved), join(d_up, d_up_moved)
        out_part = out_keep + out_moved.astype(jnp.float32)
        out_keep, out_moved = scatter_until(out_part, n_z // 2, 2)
        in_part = contract_last(d_gate, gate_weight)
        in_part, out_moved, d_up = tie((in_part, out_moved, d_up))
        out_keep, out_moved = scatter_start(out_keep + out_moved.astype(jnp.float32), 1)
        in_part = in_part + contract_last(d_up, up_weight)
        in_part, d_gate, d_up, out_moved = tie((in_part, d_gate, d_up, out_moved))
        output = (out_keep + out_moved.astype(jnp.float32)).astype(BF16)
        in_keep, in_moved = scatter_until(in_part, n_row // 2, max(n_z, 1))
        gate_grad = weight_grad(inputs_t, d_gate)
        gate_grad, in_moved, d_up = tie((gate_grad, in_moved, d_up))
        in_keep, in_moved = scatter_until(in_keep + in_moved.astype(jnp.float32), n_z // 2, 2)
        up_grad = weight_grad(inputs_t, d_up)
        up_grad, in_moved = tie((up_grad, in_moved))
        in_keep, in_moved = scatter_start(in_keep + in_moved.astype(jnp.float32), 1)
        in_grad = (in_keep + in_moved.astype(jnp.float32)).astype(BF16)
        return (output, in_grad, gate_grad, up_grad, down_grad)

    return shards


def solution(mesh):
    in_specs = (P("row", "col"), P("col", "row"), P("col", "row"), P("row", "col"), P("row", "col"))
    out_specs = (
        P("row", "col"),
        P("row", "col"),
        P("col", "row"),
        P("col", "row"),
        P("row", "col"),
    )
    shards = make_shards(mesh.shape["row"], mesh.shape["col"])
    return jax.shard_map(shards, mesh=mesh, in_specs=in_specs, out_specs=out_specs, check_vma=False)
```

```python
import functools

import jax
import jax.numpy as jnp
from jax import lax
from jax.experimental import pallas as pl
from jax.experimental.pallas import tpu as pltpu
from jax.sharding import PartitionSpec as P

BF16 = jnp.bfloat16


def contract_last(left, right):
    return lax.dot_general(
        left, right, (((1,), (1,)), ((), ())), preferred_element_type=jnp.float32
    )


def contract_first(left, right):
    return lax.dot_general(
        left, right, (((0,), (0,)), ((), ())), preferred_element_type=jnp.float32
    )


def contract_mid(left, right):
    return jnp.dot(left, right, preferred_element_type=jnp.float32)


def tile_of(size, most):
    best = size
    for tile in range(128, most + 1, 128):
        if size % tile == 0:
            best = tile
    return best


def weight_grad_kernel(left_ref, right_ref, out_ref):
    out_ref[...] = jnp.dot(
        left_ref[...], right_ref[...], preferred_element_type=jnp.float32
    ).astype(out_ref.dtype)


def weight_grad(left_t, right):
    rows, tokens = left_t.shape
    cols = right.shape[1]
    tile = tile_of(cols, 512)
    return pl.pallas_call(
        weight_grad_kernel,
        grid=(cols // tile,),
        in_specs=[
            pl.BlockSpec((rows, tokens), lambda i: (0, 0)),
            pl.BlockSpec((tokens, tile), lambda i: (0, i)),
        ],
        out_specs=pl.BlockSpec((rows, tile), lambda i: (0, i)),
        out_shape=jax.ShapeDtypeStruct((rows, cols), BF16),
        cost_estimate=pl.CostEstimate(
            flops=2 * tokens * rows * cols,
            bytes_accessed=2 * (tokens * rows + tokens * cols + rows * cols),
            transcendentals=0,
        ),
    )(left_t, right)


def gather_kernel(n_z, n_y, cores, *refs):
    count = (len(refs) - 7) // 2
    ins, outs = refs[:count], refs[count : 2 * count]
    own_sem, up_send, up_recv, down_send, down_recv, y_send, y_recv = refs[2 * count :]
    row = lax.axis_index("row")
    core = lax.rem(lax.axis_index("col"), cores)
    z, y = row // n_y, lax.rem(row, n_y)
    peers = [lax.rem(y + step, n_y) for step in range(1, n_y)]
    barrier = pltpu.get_barrier_semaphore()

    def greet(z_to, y_to):
        pl.semaphore_signal(
            barrier, inc=1, device_id={"row": z_to * n_y + y_to}, device_id_type=pl.DeviceIdType.MESH
        )

    @pl.when(z < n_z - 1)
    def _():
        greet(z + 1, y)

    @pl.when(z > 0)
    def _():
        greet(z - 1, y)

    for peer in peers:
        greet(z, peer)

    ends = jnp.where(z > 0, 1, 0) + jnp.where(z < n_z - 1, 1, 0)
    pl.semaphore_wait(barrier, ends + len(peers))

    def slot(z_of, y_of):
        return lax.rem(y_of + core * (n_y // 2), n_y) * n_z + z_of

    def copy(item, source, z_of, sems, z_to, y_to):
        target = outs[item].at[slot(z_of, y)]
        return pltpu.make_async_remote_copy(
            src_ref=target if source is None else source,
            dst_ref=target,
            send_sem=sems[0],
            recv_sem=sems[1],
            device_id={"row": z_to * n_y + y_to},
            device_id_type=pl.DeviceIdType.MESH,
        )

    def up(item, step):
        source = ins[item] if step == 0 else None
        sems = (up_send.at[item, step], up_recv.at[item, step])
        return copy(item, source, z - step, sems, z + 1, y)

    def down(item, step):
        source = ins[item] if step == 0 else None
        sems = (down_send.at[item, step], down_recv.at[item, step])
        return copy(item, source, z + step, sems, z - 1, y)

    def across(item, offset, z_of, own):
        source = ins[item] if own else None
        place = lax.rem(z_of + n_z, n_z)
        sems = (y_send.at[item, offset, place], y_recv.at[item, offset, place])
        return copy(item, source, z_of, sems, z, peers[offset])

    def sends(item, step, act):
        @pl.when((z < n_z - 1) & (z >= step))
        def _():
            act(up(item, step))

        @pl.when((z > 0) & (z + step <= n_z - 1))
        def _():
            act(down(item, step))

        for offset in range(n_y - 1):
            if step == 0:
                act(across(item, offset, z, True))
            else:

                @pl.when(z >= step)
                def _():
                    act(across(item, offset, z - step, False))

                @pl.when(z + step <= n_z - 1)
                def _():
                    act(across(item, offset, z + step, False))

    local = [
        pltpu.make_async_copy(ins[item], outs[item].at[slot(z, y)], own_sem.at[item])
        for item in range(count)
    ]
    for item in range(count):
        sends(item, 0, lambda c: c.start())
        local[item].start()
    for item in range(count):
        for step in range(1, n_z):

            @pl.when(z >= step)
            def _():
                up(item, step - 1).wait_recv()

            @pl.when(z + step <= n_z - 1)
            def _():
                down(item, step - 1).wait_recv()

            sends(item, step, lambda c: c.start())
    for item in range(count):
        local[item].wait()
        for offset in range(n_y - 1):
            for z_of in range(n_z):
                across(item, offset, z_of, False).wait_recv()
        for step in range(n_z):
            sends(item, step, lambda c: c.wait_send())


def gather_rows(n_z, n_y, cores, call, *arrays):
    count = len(arrays)
    line = pltpu.SemaphoreType.DMA((count, n_z))
    side = pltpu.SemaphoreType.DMA((count, n_y, n_z))
    shape = arrays[0].shape
    out = pl.pallas_call(
        functools.partial(gather_kernel, n_z, n_y, cores),
        out_shape=[jax.ShapeDtypeStruct((n_z * n_y,) + shape, a.dtype) for a in arrays],
        in_specs=[pl.BlockSpec(memory_space=pl.ANY)] * count,
        out_specs=[pl.BlockSpec(memory_space=pl.ANY)] * count,
        scratch_shapes=[pltpu.SemaphoreType.DMA((count,)), line, line, line, line, side, side],
        cost_estimate=pl.CostEstimate(
            flops=0, bytes_accessed=8 * n_z * n_y * count * arrays[0].size, transcendentals=0
        ),
        compiler_params=pltpu.CompilerParams(collective_id=call, has_side_effects=True),
    )(*arrays)
    return [value.reshape(-1, shape[1]) for value in out]


def make_shards(n_row, n_col):
    cores = 2 if n_col % 2 == 0 else 1
    n_x = n_col // cores
    n_y = n_x if n_row % n_x == 0 and n_x % 2 == 0 else (2 if n_row % 2 == 0 else 1)
    n_z = n_row // n_y
    half = cores == 2 and n_y % 2 == 0

    def row_swap(value, bit):
        return lax.ppermute(value, "row", [(r, r ^ bit) for r in range(n_row)])

    def x_move(value, step):
        pairs = [
            (x * cores + k, (x + step) % n_x * cores + k) for x in range(n_x) for k in range(cores)
        ]
        return lax.ppermute(value, "col", pairs)

    def core_move(value):
        pairs = [(x * cores + k, x * cores + 1 - k) for x in range(n_x) for k in range(cores)]
        return lax.ppermute(value, "col", pairs)

    def scatter_start(total, bit):
        row = lax.axis_index("row")
        core = lax.rem(lax.axis_index("col"), cores)
        z, y = row // n_y, lax.rem(row, n_y)
        slot = lax.rem(y + core * (n_y // 2), n_y) * n_z + z
        rows = total.shape[0] // 2
        side = (slot // bit) % 2
        keep = lax.dynamic_slice_in_dim(total, side * rows, rows)
        send = lax.dynamic_slice_in_dim(total, (1 - side) * rows, rows).astype(BF16)
        return keep, row_swap(send, bit // n_z if bit >= n_z else bit * n_y)

    def gather_step(value, bit):
        arrived = row_swap(value, bit // n_z if bit >= n_z else bit * n_y)

        def both(arrived):
            row = lax.axis_index("row")
            core = lax.rem(lax.axis_index("col"), cores)
            slot = lax.rem(lax.rem(row, n_y) + core * (n_y // 2), n_y) * n_z + row // n_y
            lower = (slot // bit) % 2 == 0
            return jnp.concatenate(
                [jnp.where(lower, value, arrived), jnp.where(lower, arrived, value)], axis=0
            )

        return arrived, both

    def scatter_until(total, bit, last):
        while True:
            keep, arrived = scatter_start(total, bit)
            if bit == last:
                return keep, arrived
            total = keep + arrived.astype(jnp.float32)
            bit //= 2

    def sum_core(part, dtype):
        if cores == 1:
            return part
        if half:
            rows = part.shape[0] // 2
            return part[:rows] + core_move(part[rows:].astype(dtype)).astype(jnp.float32)
        return part + core_move(part)

    def send_x(mine):
        return [x_move(mine, step) for step in range(1, n_x)]

    def add_all(mine, moved):
        for value in moved:
            mine = mine + value.astype(jnp.float32)
        return mine

    def join(share, moved):
        return share if moved is None else jnp.concatenate([share, moved], axis=0)

    def core_send(share):
        return core_move(share) if half else None

    tie = lax.optimization_barrier

    def shards(tokens_in, gate_weight, up_weight, down_weight, out_grad):
        (inputs_all,) = gather_rows(n_z, n_y, cores, 0, tokens_in)
        inputs_all, out_grad = tie((inputs_all, out_grad))
        arrived, both = gather_step(out_grad, 1)
        gate_part = contract_mid(inputs_all, gate_weight)
        inputs_all, gate_part, arrived = tie((inputs_all, gate_part, arrived))
        grad_all, bit = both(arrived), 2
        arrived, both = gather_step(grad_all, bit)
        gate_mine = sum_core(gate_part, BF16)
        gate_moved = send_x(gate_mine.astype(BF16))
        up_mine = sum_core(contract_mid(inputs_all, up_weight), jnp.float32)
        arrived, up_sent = tie((arrived, up_mine.astype(BF16)))
        up_moved = send_x(up_sent)
        grad_all = both(arrived)
        inputs_t = inputs_all.T
        while bit < n_row // 2:
            bit *= 2
            arrived, both = gather_step(grad_all, bit)
            arrived, inputs_t = tie((arrived, inputs_t))
            grad_all = both(arrived)
        d_part = contract_last(grad_all, down_weight)
        d_mine = sum_core(d_part, jnp.float32)
        d_sent, gate_moved, up_moved, inputs_t = tie(
            (d_mine.astype(BF16), gate_moved, up_moved, inputs_t)
        )
        d_moved = send_x(d_sent)
        gate_pre, up_pre = add_all(gate_mine, gate_moved), add_all(up_mine, up_moved)
        sigma = jax.nn.sigmoid(gate_pre)
        activated = gate_pre * sigma
        share = (activated * up_pre).astype(BF16)
        hidden = join(share, core_send(share))
        output_part = contract_mid(hidden, down_weight)
        d_moved, output_part = tie((d_moved, output_part))
        out_keep, out_moved = scatter_until(output_part, n_row // 2, max(n_z, 1))
        d_hidden = add_all(d_mine, d_moved)
        d_gate = (d_hidden * up_pre * sigma * (1.0 + gate_pre * (1.0 - sigma))).astype(BF16)
        d_up = (d_hidden * activated).astype(BF16)
        d_gate, d_up, hidden = tie((d_gate, d_up, hidden))
        d_gate_moved, d_up_moved = core_send(d_gate), core_send(d_up)
        down_grad = contract_first(hidden, grad_all).astype(BF16)
        d_gate_moved, d_up_moved, out_moved, down_grad = tie(
            (d_gate_moved, d_up_moved, out_moved, down_grad)
        )
        d_gate, d_up = join(d_gate, d_gate_moved), join(d_up, d_up_moved)
        out_part = out_keep + out_moved.astype(jnp.float32)
        out_keep, out_moved = scatter_until(out_part, n_z // 2, 2)
        in_part = contract_last(d_gate, gate_weight)
        in_part, out_moved, d_up = tie((in_part, out_moved, d_up))
        out_keep, out_moved = scatter_start(out_keep + out_moved.astype(jnp.float32), 1)
        in_part = in_part + contract_last(d_up, up_weight)
        in_part, d_gate, d_up, out_moved = tie((in_part, d_gate, d_up, out_moved))
        output = (out_keep + out_moved.astype(jnp.float32)).astype(BF16)
        in_keep, in_moved = scatter_until(in_part, n_row // 2, max(n_z, 1))
        gate_grad = weight_grad(inputs_t, d_gate)
        gate_grad, in_moved, d_up = tie((gate_grad, in_moved, d_up))
        in_keep, in_moved = scatter_until(in_keep + in_moved.astype(jnp.float32), n_z // 2, 2)
        up_grad = weight_grad(inputs_t, d_up)
        up_grad, in_moved = tie((up_grad, in_moved))
        in_keep, in_moved = scatter_start(in_keep + in_moved.astype(jnp.float32), 1)
        in_grad = (in_keep + in_moved.astype(jnp.float32)).astype(BF16)
        return (output, in_grad, gate_grad, up_grad, down_grad)

    return shards


def solution(mesh):
    in_specs = (P("row", "col"), P("col", "row"), P("col", "row"), P("row", "col"), P("row", "col"))
    out_specs = (
        P("row", "col"),
        P("row", "col"),
        P("col", "row"),
        P("col", "row"),
        P("row", "col"),
    )
    shards = make_shards(mesh.shape["row"], mesh.shape["col"])
    return jax.shard_map(shards, mesh=mesh, in_specs=in_specs, out_specs=out_specs, check_vma=False)
```
